32 devices in a mesh: ctx: 8 (over z, y), head: 4 (over x, core).
Axes of the slice: x: 2, y: 2, z: 4, core: 2. Of those that a mesh axis runs over, the one named last changes fastest.
Arguments:
- tokens: bfloat16 [2048, 6144], P('ctx'), may hold values from -6 to 6
- query_heads: bfloat16 [2048, 4096], P('ctx', 'head'), may hold values from -6 to 6
- key_heads: bfloat16 [2048, 4096], P('ctx', 'head'), may hold values from -6 to 6
- w_value: bfloat16 [6144, 4096], P('ctx', 'head'), may hold values from -0.078125 to 0.078125
- norm_gain: float32 [4096], P('head'), may hold values from 0.5 to 1.5
Outputs:
- attn_out: bfloat16 [2048, 4096], P('ctx', 'head')
The draws below stay inside these ranges and needn't reach their ends.
All inputs are finite; a program needn't handle non-finite values.
Results may differ from the reference program's by a relative error of at most 0.0054.
Values may be sent and summed in bfloat16 or wider, within the bound.
A program may use at most 128 MiB of HBM per device.

```python
import jax
import jax.numpy as jnp
from jax import lax

D = 6144
HEADS = 32
HD = 128
BLOCK = 256
TOKENS = 2048
HC = 4096


def block_levels(key, shape, split, low, high):
    def one(position, shards_of):
        heights = jax.random.uniform(jax.random.fold_in(jax.random.fold_in(key, 6), position), (shards_of,), jnp.float32, low / len(split), high / len(split))
        return jnp.repeat(jnp.exp(heights), shape[position] // shards_of).reshape((-1,) + (1,) * (len(shape) - position - 1))

    gain = one(*split[0])
    for cut in split[1:]:
        gain = gain * one(*cut)
    return gain


def normal_values(key, shape, spread, most, split=(), kind=jnp.bfloat16):
    array = spread * jax.random.normal(key, shape, jnp.float32)
    if split:
        array = array * block_levels(key, shape, split, -0.22, 0.18)
    return jnp.clip(array, -most, most).astype(kind)


def setup_inputs(seed: int = 0) -> dict:
    streams_of = jax.random.split(jax.random.key(seed), 6)
    return {
        "tokens": normal_values(streams_of[0], (TOKENS, D), 1.0, 6.0, ((0, 8),)),
        "query_heads": normal_values(streams_of[1], (TOKENS, HC), 1.0, 6.0, ((0, 8), (1, 4))),
        "key_heads": normal_values(streams_of[2], (TOKENS, HC), 1.0, 6.0, ((0, 8), (1, 4))),
        "w_value": normal_values(streams_of[3], (D, HC), D ** -0.5, 0.078125, ((0, 8), (1, 4))),
        "norm_gain": jnp.clip(1.0 + 0.1 * jax.random.normal(streams_of[4], (HC,), jnp.float32), 0.5, 1.5),
    }


def reference(tokens, query_heads, key_heads, w_value, norm_gain):
    pre_value = jnp.dot(tokens, w_value, preferred_element_type=jnp.float32)
    value_heads = jax.nn.silu(pre_value).astype(jnp.bfloat16)
    block_count = TOKENS // BLOCK
    shaped_q = query_heads.reshape(block_count, BLOCK, HEADS, HD).astype(jnp.float32)
    shaped_k = key_heads.reshape(block_count, BLOCK, HEADS, HD).astype(jnp.float32)
    shaped_v = value_heads.reshape(block_count, BLOCK, HEADS, HD).astype(jnp.float32)
    causal = jnp.tril(jnp.ones((BLOCK, BLOCK), jnp.bool_))

    def one_block(carried, inputs):
        block_q, block_k, block_v = inputs
        inter = jnp.einsum('shd,hde->she', block_q, carried, precision=lax.Precision.HIGHEST)
        scores = jnp.einsum('shd,thd->hst', block_q, block_k, precision=lax.Precision.HIGHEST)
        scores = jnp.where(causal[None], scores, jnp.float32(0.0)).astype(jnp.bfloat16)
        intra = jnp.einsum('hst,thd->shd', scores.astype(jnp.float32), block_v, precision=lax.Precision.HIGHEST)
        local_state = jnp.einsum('shd,she->hde', block_k, block_v, precision=lax.Precision.HIGHEST)
        return (carried + local_state, inter + intra)
    initial = jnp.zeros((HEADS, HD, HD), jnp.float32)
    _, attended = lax.scan(one_block, initial, (shaped_q, shaped_k, shaped_v))
    attended = attended.reshape(TOKENS, HEADS, HD)
    mean_square = lax.optimization_barrier(jnp.mean(attended * attended, axis=2, keepdims=True))
    normed = attended * lax.rsqrt(mean_square + 1e-05) * norm_gain.reshape(1, HEADS, HD)
    return normed.reshape(TOKENS, HEADS * HD).astype(jnp.bfloat16)
```

```python
import functools

import jax
import jax.numpy as jnp
from jax import lax
from jax.experimental import pallas as pl
from jax.experimental.pallas import tpu as pltpu
from jax.sharding import PartitionSpec as P

MESH = pl.DeviceIdType.MESH
F32 = jnp.float32
BF16 = jnp.bfloat16
CW = 256

HD = 128
BLOCK = 256


def prefix(part, axis, combine, identity):
    place = lax.axis_index(axis)
    gathered = lax.all_gather(part, axis)
    state = jnp.zeros_like(part) + jnp.asarray(identity, part.dtype)

    def one(lap, state):
        return combine(state, lax.dynamic_index_in_dim(gathered, lap, 0, False))

    return lax.fori_loop(0, place, one, state)


def add_states(earlier, later):
    return earlier + later


def plain(tokens, query_heads, key_heads, w_value, norm_gain):
    token_count = tokens.shape[0]
    width = w_value.shape[1]
    heads_here = width // HD
    full_weight = lax.all_gather(w_value, "ctx", axis=0, tiled=True)
    pre_value = jnp.dot(tokens, full_weight, preferred_element_type=jnp.float32)
    value_heads = jax.nn.silu(pre_value).astype(jnp.bfloat16)
    block_count = token_count // BLOCK
    block_shape = (block_count, BLOCK, heads_here, HD)
    shaped_q = query_heads.reshape(block_shape)
    shaped_k = key_heads.reshape(block_shape)
    shaped_v = value_heads.reshape(block_shape)
    local_states = jnp.einsum(
        "bshd,bshe->bhde", shaped_k, shaped_v, preferred_element_type=jnp.float32
    )
    device_state = jnp.sum(local_states, axis=0)
    running_sum = jnp.cumsum(local_states, axis=0)
    before_block = jnp.concatenate([jnp.zeros_like(local_states), running_sum[:-1]], axis=0)
    earlier = prefix(device_state, "ctx", add_states, jnp.zeros_like(device_state))
    prefix_state = earlier[None] + before_block
    inter = jnp.einsum(
        "bshd,bhde->bshe",
        shaped_q.astype(jnp.float32),
        prefix_state,
        precision=lax.Precision.HIGHEST,
    )
    scores = jnp.einsum("bshd,bthd->bhst", shaped_q, shaped_k, preferred_element_type=jnp.float32)
    causal = jnp.tril(jnp.ones((BLOCK, BLOCK), jnp.bool_))
    scores = jnp.where(causal[None, None], scores, jnp.float32(0.0)).astype(jnp.bfloat16)
    intra = jnp.einsum("bhst,bthd->bshd", scores, shaped_v, preferred_element_type=jnp.float32)
    attended = (inter + intra).reshape(token_count, heads_here, HD)
    mean_square = jnp.mean(attended * attended, axis=2, keepdims=True)
    normed = attended * lax.rsqrt(mean_square + 1e-05) * norm_gain.reshape(1, heads_here, HD)
    return normed.reshape(token_count, width).astype(jnp.bfloat16)


def fused_kernel(
    nz, chunks, tokens, query, key, weight, gain, out,
    tok, wbuf, p_send, p_recv, acc, scores, value, att, state, state_in, t_send, t_recv, pre_send, pre,
    local_sem, w_ss, w_rs, tok_ss, tok_rs, x_ss, x_rs, core_ss, core_rs, p_ss, p_rs,
    s_ss, s_rs, t_ss, t_rs, e_ss, e_rs,
):
    ctx = lax.axis_index("ctx")
    head = lax.axis_index("head")
    zi, yi = ctx // 2, ctx % 2
    rows = tokens.shape[0]
    depth = weight.shape[0]
    slice_width = 2 * depth
    quarter = rows // 4

    def along_z(d):
        return lax.rem(zi + d, nz)

    def device_z(d):
        return (along_z(d) * 2 + yi, head)

    pair = (zi * 2 + 1 - yi, head)
    core_peer = head + 1 - 2 * (head % 2)
    x_peer = lax.rem(head + 2, 4)

    def remote(src, dst, ss, rs, device):
        return pltpu.make_async_remote_copy(
            src_ref=src, dst_ref=dst, send_sem=ss, recv_sem=rs, device_id=device, device_id_type=MESH
        )

    def columns(z):
        return pl.ds(pl.multiple_of(z * slice_width, 128), slice_width)

    def token_rows(h):
        return pl.ds(pl.multiple_of(h * quarter, quarter), quarter)

    own_rows = pl.ds(pl.multiple_of(yi * depth, depth), depth)

    own_tokens = pltpu.make_async_copy(tokens.at[:, columns(zi)], tok.at[zi], local_sem.at[0])
    own_tokens.start()
    own_weights = []
    for j in range(chunks):
        own_weights.append(
            pltpu.make_async_copy(
                weight.at[:, pl.ds(j * CW, CW)], wbuf.at[j, own_rows, :], local_sem.at[1 + j]
            )
        )
        own_weights[j].start()

    barrier = pltpu.get_barrier_semaphore()
    greeted = [device_z(d) for d in range(1, nz)] + [pair, (ctx, core_peer), (ctx, x_peer)]
    for device in greeted:
        pl.semaphore_signal(barrier, inc=1, device_id=device, device_id_type=MESH)
    pl.semaphore_wait(barrier, len(greeted))

    token_copies = {}
    for d in range(nz - 1, 0, -1):
        token_copies[d] = remote(
            tokens.at[token_rows(head), columns(along_z(d))],
            tok.at[zi, token_rows(head), :],
            tok_ss.at[d], tok_rs.at[d], device_z(d),
        )
        token_copies[d].start()
    w_copies = []
    for j in range(chunks):
        w_copies.append(
            remote(
                weight.at[:, pl.ds(j * CW, CW)], wbuf.at[j, own_rows, :], w_ss.at[j], w_rs.at[j], pair
            )
        )
        w_copies[j].start()

    row = lax.broadcasted_iota(jnp.int32, (rows, rows), 0)
    column = lax.broadcasted_iota(jnp.int32, (rows, rows), 1)
    causal = column <= row
    for hd in range(2 * chunks):
        lanes = pl.ds(hd * HD, HD)
        full = lax.dot_general(
            query[:, lanes], key[:, lanes], (((1,), (1,)), ((), ())), preferred_element_type=F32
        )
        scores[hd] = jnp.where(causal, full, 0.0).astype(BF16)

    x_copies, core_copies = {}, {}
    order = list(range(1, nz))
    for d in order:
        source = lax.rem(zi - d + nz, nz)
        mine = tok.at[source, token_rows(head), :]
        token_copies[d].wait_recv()
        x_copies[d] = remote(mine, mine, x_ss.at[d], x_rs.at[d], (ctx, x_peer))
        x_copies[d].start()
        core_copies[d, 0] = remote(mine, mine, core_ss.at[0, d], core_rs.at[0, d], (ctx, core_peer))
        core_copies[d, 0].start()
    for d in order:
        source = lax.rem(zi - d + nz, nz)
        other = tok.at[source, token_rows(x_peer), :]
        x_copies[d].wait_recv()
        core_copies[d, 1] = remote(other, other, core_ss.at[1, d], core_rs.at[1, d], (ctx, core_peer))
        core_copies[d, 1].start()
    for d in order:
        core_copies[d, 0].wait_recv()
        core_copies[d, 1].wait_recv()
    own_tokens.wait()

    p_copies = {}
    for j in range(chunks):
        own_weights[j].wait()
        w_copies[j].wait_recv()
        for d in range(nz - 1, 0, -1):
            part = jnp.dot(tok[along_z(d)], wbuf[j], preferred_element_type=F32)
            p_send[d - 1, j] = part.astype(BF16)
            p_copies[d, j] = remote(
                p_send.at[d - 1, j], p_recv.at[d - 1, j], p_ss.at[d - 1, j], p_rs.at[d - 1, j], device_z(d)
            )
            p_copies[d, j].start()
        acc[j] = jnp.dot(tok[zi], wbuf[j], preferred_element_type=F32)

    s_copies = [
        remote(state.at[j, 1 - yi], state_in.at[j], s_ss.at[j], s_rs.at[j], pair) for j in range(chunks)
    ]
    e_copies = [
        remote(pre_send.at[j], pre.at[j, yi], e_ss.at[j], e_rs.at[j], pair) for j in range(chunks)
    ]

    def t_copy(d, j):
        return remote(t_send.at[j], t_recv.at[d - 1, j], t_ss.at[d - 1, j], t_rs.at[d - 1, j], device_z(d))

    def values(j):
        total = acc[j]
        for d in range(1, nz):
            p_copies[d, j].wait_recv()
            total = total + p_recv[d - 1, j].astype(F32)
        value[j] = (total / (1.0 + jnp.exp(-total))).astype(BF16)
        for i in range(2):
            hd = 2 * j + i
            state[j, i] = lax.dot_general(
                key[:, pl.ds(hd * HD, HD)], value[j, :, pl.ds(i * HD, HD)],
                (((0,), (0,)), ((), ())), preferred_element_type=F32,
            )
        s_copies[j].start()
        for i in range(2):
            att[2 * j + i] = jnp.dot(
                scores[2 * j + i], value[j, :, pl.ds(i * HD, HD)], preferred_element_type=F32
            )

    def pair_sum(j):
        s_copies[j].wait_recv()
        t_send[j] = (state[j, yi] + state_in[j]).astype(BF16)
        for d in range(1, nz):
            @pl.when(zi + d < nz)
            def _():
                t_copy(d, j).start()

    def earlier(j):
        pre_send[j] = jnp.zeros((HD, HD), F32)
        for d in range(1, nz):
            @pl.when(zi - d >= 0)
            def _():
                t_copy(d, j).wait_recv()
                pre_send[j] = pre_send[j] + t_recv[d - 1, j].astype(F32)
        second = yi.astype(F32)
        before = pre_send[j]
        pre[j, yi] = before + second * state_in[j]
        pre_send[j] = before + (1.0 - second) * state[j, yi]
        e_copies[j].start()

    def finish(j):
        e_copies[j].wait_recv()
        for i in range(2):
            lanes = pl.ds((2 * j + i) * HD, HD)
            whole = pre[j, i]
            high = whole.astype(BF16)
            low = (whole - high.astype(F32)).astype(BF16)
            q = query[:, lanes]
            attended = (
                att[2 * j + i]
                + jnp.dot(q, high, preferred_element_type=F32)
                + jnp.dot(q, low, preferred_element_type=F32)
            )
            mean_square = jnp.mean(attended * attended, axis=1, keepdims=True)
            out[:, lanes] = (attended * lax.rsqrt(mean_square + 1e-05) * gain[:, lanes]).astype(BF16)

    stages = (values, pair_sum, earlier, finish)
    for step in range(chunks + len(stages) - 1):
        for lag, stage in enumerate(stages):
            if 0 <= step - lag < chunks:
                stage(step - lag)

    for copy in [*token_copies.values(), *w_copies, *x_copies.values(), *core_copies.values()]:
        copy.wait_send()
    for copy in [*p_copies.values(), *s_copies, *e_copies]:
        copy.wait_send()
    for j in range(chunks):
        for d in range(1, nz):
            @pl.when(zi + d < nz)
            def _():
                t_copy(d, j).wait_send()


def fused(n, tokens, query, key, weight, gain):
    rows = tokens.shape[0]
    depth, width = weight.shape
    nz = n // 2
    chunks = width // CW
    dma = pltpu.SemaphoreType.DMA
    hbm = pl.BlockSpec(memory_space=pl.ANY)
    vmem = pl.BlockSpec(memory_space=pltpu.VMEM)
    others = nz - 1
    return pl.pallas_call(
        functools.partial(fused_kernel, nz, chunks),
        out_shape=jax.ShapeDtypeStruct((rows, width), BF16),
        in_specs=[hbm, vmem, vmem, hbm, vmem],
        out_specs=vmem,
        scratch_shapes=[
            pltpu.VMEM((nz, rows, 2 * depth), BF16),
            pltpu.VMEM((chunks, 2 * depth, CW), BF16),
            pltpu.VMEM((others, chunks, rows, CW), BF16),
            pltpu.VMEM((others, chunks, rows, CW), BF16),
            pltpu.VMEM((chunks, rows, CW), F32),
            pltpu.VMEM((2 * chunks, rows, rows), BF16),
            pltpu.VMEM((chunks, rows, CW), BF16),
            pltpu.VMEM((2 * chunks, rows, HD), F32),
            pltpu.VMEM((chunks, 2, HD, HD), F32),
            pltpu.VMEM((chunks, HD, HD), F32),
            pltpu.VMEM((chunks, HD, HD), BF16),
            pltpu.VMEM((others, chunks, HD, HD), BF16),
            pltpu.VMEM((chunks, HD, HD), F32),
            pltpu.VMEM((chunks, 2, HD, HD), F32),
            dma((1 + chunks,)),
            dma((chunks,)), dma((chunks,)),
            dma((nz,)), dma((nz,)),
            dma((nz,)), dma((nz,)),
            dma((2, nz)), dma((2, nz)),
            dma((others, chunks)), dma((others, chunks)),
            dma((chunks,)), dma((chunks,)),
            dma((others, chunks)), dma((others, chunks)),
            dma((chunks,)), dma((chunks,)),
        ],
        compiler_params=pltpu.CompilerParams(
            collective_id=0, has_side_effects=True, vmem_limit_bytes=48 << 20
        ),
    )(tokens, query, key, weight, gain.reshape(1, width))


def on_device(n, heads, tokens, query_heads, key_heads, w_value, norm_gain):
    rows = tokens.shape[0]
    depth, width = w_value.shape
    fits = n % 2 == 0 and heads == 4 and rows == BLOCK and depth % 128 == 0 and width % CW == 0 and n <= 16
    if fits:
        return fused(n, tokens, query_heads, key_heads, w_value, norm_gain)
    return plain(tokens, query_heads, key_heads, w_value, norm_gain)


def solution(mesh):
    return jax.shard_map(
        functools.partial(on_device, mesh.shape["ctx"], mesh.shape["head"]),
        mesh=mesh,
        in_specs=(P("ctx", None), P("ctx", "head"), P("ctx", "head"), P("ctx", "head"), P("head")),
        out_specs=P("ctx", "head"),
        check_vma=False,
    )
```

```python
import functools

import jax
import jax.numpy as jnp
from jax import lax
from jax.experimental import pallas as pl
from jax.experimental.pallas import tpu as pltpu
from jax.sharding import PartitionSpec as P

MESH = pl.DeviceIdType.MESH
F32 = jnp.float32
BF16 = jnp.bfloat16
CW = 256
W_AHEAD = 2
ORDER = (1, 3, 2)

HD = 128
BLOCK = 256


def prefix(part, axis, combine, identity):
    place = lax.axis_index(axis)
    gathered = lax.all_gather(part, axis)
    state = jnp.zeros_like(part) + jnp.asarray(identity, part.dtype)

    def one(lap, state):
        return combine(state, lax.dynamic_index_in_dim(gathered, lap, 0, False))

    return lax.fori_loop(0, place, one, state)


def add_states(earlier, later):
    return earlier + later


def plain(tokens, query_heads, key_heads, w_value, norm_gain):
    token_count = tokens.shape[0]
    width = w_value.shape[1]
    heads_here = width // HD
    full_weight = lax.all_gather(w_value, "ctx", axis=0, tiled=True)
    pre_value = jnp.dot(tokens, full_weight, preferred_element_type=jnp.float32)
    value_heads = jax.nn.silu(pre_value).astype(jnp.bfloat16)
    block_count = token_count // BLOCK
    block_shape = (block_count, BLOCK, heads_here, HD)
    shaped_q = query_heads.reshape(block_shape)
    shaped_k = key_heads.reshape(block_shape)
    shaped_v = value_heads.reshape(block_shape)
    local_states = jnp.einsum(
        "bshd,bshe->bhde", shaped_k, shaped_v, preferred_element_type=jnp.float32
    )
    device_state = jnp.sum(local_states, axis=0)
    running_sum = jnp.cumsum(local_states, axis=0)
    before_block = jnp.concatenate([jnp.zeros_like(local_states), running_sum[:-1]], axis=0)
    earlier = prefix(device_state, "ctx", add_states, jnp.zeros_like(device_state))
    prefix_state = earlier[None] + before_block
    inter = jnp.einsum(
        "bshd,bhde->bshe",
        shaped_q.astype(jnp.float32),
        prefix_state,
        precision=lax.Precision.HIGHEST,
    )
    scores = jnp.einsum("bshd,bthd->bhst", shaped_q, shaped_k, preferred_element_type=jnp.float32)
    causal = jnp.tril(jnp.ones((BLOCK, BLOCK), jnp.bool_))
    scores = jnp.where(causal[None, None], scores, jnp.float32(0.0)).astype(jnp.bfloat16)
    intra = jnp.einsum("bhst,bthd->bshd", scores, shaped_v, preferred_element_type=jnp.float32)
    attended = (inter + intra).reshape(token_count, heads_here, HD)
    mean_square = jnp.mean(attended * attended, axis=2, keepdims=True)
    normed = attended * lax.rsqrt(mean_square + 1e-05) * norm_gain.reshape(1, heads_here, HD)
    return normed.reshape(token_count, width).astype(jnp.bfloat16)


def fused_kernel(
    nz, chunks, tokens, query, key, weight, gain, out,
    tok, wbuf, p_send, p_recv, far, far_send, far_recv, acc, scores, value, att,
    state, state_in, t_send, u_send, t_recv, u_recv, pre_send, pre,
    local_sem, w_ss, w_rs, tok_ss, tok_rs, x_ss, x_rs, core_ss, core_rs, p_ss, p_rs, f_ss, f_rs,
    s_ss, s_rs, t_ss, t_rs, u_ss, u_rs, e_ss, e_rs,
):
    ctx = lax.axis_index("ctx")
    head = lax.axis_index("head")
    zi, yi = ctx // 2, ctx % 2
    rows = tokens.shape[0]
    depth = weight.shape[0]
    slice_width = 2 * depth
    quarter = rows // 4

    z_peers = {1: zi + 1 - 2 * (zi % 2), 2: lax.rem(zi + 2, nz), 3: nz - 1 - zi}

    def device_z(m):
        return (z_peers[m] * 2 + yi, head)

    pair = (zi * 2 + 1 - yi, head)
    core_peer = head + 1 - 2 * (head % 2)
    x_peer = lax.rem(head + 2, 4)

    def remote(src, dst, ss, rs, device):
        return pltpu.make_async_remote_copy(
            src_ref=src, dst_ref=dst, send_sem=ss, recv_sem=rs, device_id=device, device_id_type=MESH
        )

    def columns(z):
        return pl.ds(pl.multiple_of(z * slice_width, 128), slice_width)

    def token_rows(h):
        return pl.ds(pl.multiple_of(h * quarter, quarter), quarter)

    own_rows = pl.ds(pl.multiple_of(yi * depth, depth), depth)

    own_tokens = pltpu.make_async_copy(tokens.at[:, columns(zi)], tok.at[zi], local_sem.at[0])
    own_tokens.start()
    own_weights = []
    for j in range(chunks):
        own_weights.append(
            pltpu.make_async_copy(
                weight.at[:, pl.ds(j * CW, CW)], wbuf.at[j, own_rows, :], local_sem.at[1 + j]
            )
        )
        own_weights[j].start()

    barrier = pltpu.get_barrier_semaphore()
    greeted = [device_z(m) for m in z_peers] + [pair, (ctx, core_peer), (ctx, x_peer)]
    for device in greeted:
        pl.semaphore_signal(barrier, inc=1, device_id=device, device_id_type=MESH)
    pl.semaphore_wait(barrier, len(greeted))

    w_copies = []
    for j in range(chunks):
        w_copies.append(
            remote(
                weight.at[:, pl.ds(j * CW, CW)], wbuf.at[j, own_rows, :], w_ss.at[j], w_rs.at[j], pair
            )
        )
    for j in range(min(W_AHEAD, chunks)):
        w_copies[j].start()
    token_copies = {}
    for m in ORDER:
        token_copies[m] = remote(
            tokens.at[token_rows(head), columns(z_peers[m])],
            tok.at[zi, token_rows(head), :],
            tok_ss.at[m], tok_rs.at[m], device_z(m),
        )
        token_copies[m].start()

    row = lax.broadcasted_iota(jnp.int32, (rows, rows), 0)
    column = lax.broadcasted_iota(jnp.int32, (rows, rows), 1)
    causal = column <= row
    for hd in range(2 * chunks):
        lanes = pl.ds(hd * HD, HD)
        full = lax.dot_general(
            query[:, lanes], key[:, lanes], (((1,), (1,)), ((), ())), preferred_element_type=F32
        )
        scores[hd] = jnp.where(causal, full, 0.0).astype(BF16)

    x_copies, core_copies = {}, {}
    for m in ORDER:
        mine = tok.at[z_peers[m], token_rows(head), :]
        token_copies[m].wait_recv()
        x_copies[m] = remote(mine, mine, x_ss.at[m], x_rs.at[m], (ctx, x_peer))
        x_copies[m].start()
        core_copies[m, 0] = remote(mine, mine, core_ss.at[0, m], core_rs.at[0, m], (ctx, core_peer))
        core_copies[m, 0].start()
    for m in ORDER:
        other = tok.at[z_peers[m], token_rows(x_peer), :]
        x_copies[m].wait_recv()
        core_copies[m, 1] = remote(other, other, core_ss.at[1, m], core_rs.at[1, m], (ctx, core_peer))
        core_copies[m, 1].start()

    p_copies = [remote(p_send.at[j], p_recv.at[j], p_ss.at[j], p_rs.at[j], device_z(1)) for j in range(chunks)]
    far_copies = [
        remote(far_send.at[j], far_recv.at[j], f_ss.at[j], f_rs.at[j], device_z(2)) for j in range(chunks)
    ]

    def tokens_of(m, j):
        if j == 0:
            core_copies[m, 0].wait_recv()
            core_copies[m, 1].wait_recv()
        return tok[z_peers[m]]

    def near_parts(j):
        own_weights[j].wait()
        w_copies[j].wait_recv()
        if j + W_AHEAD < chunks:
            w_copies[j + W_AHEAD].start()
        for i, m in enumerate((1, 3)):
            p_send[j, i] = jnp.dot(tokens_of(m, j), wbuf[j], preferred_element_type=F32).astype(BF16)
        p_copies[j].start()
        if j == 0:
            own_tokens.wait()
        far[j] = jnp.dot(tokens_of(2, j), wbuf[j], preferred_element_type=F32)
        acc[j] = jnp.dot(tok[zi], wbuf[j], preferred_element_type=F32)

    def far_parts(j):
        p_copies[j].wait_recv()
        far_send[j] = (far[j] + p_recv[j, 1].astype(F32)).astype(BF16)
        far_copies[j].start()

    for step in range(chunks + 1):
        if step < chunks:
            near_parts(step)
        if step >= 1:
            far_parts(step - 1)

    s_copies = [
        remote(state.at[j, 1 - yi], state_in.at[j], s_ss.at[j], s_rs.at[j], pair) for j in range(chunks)
    ]
    e_copies = [
        remote(pre_send.at[j], pre.at[j, yi], e_ss.at[j], e_rs.at[j], pair) for j in range(chunks)
    ]

    t_copies = [remote(t_send.at[j], t_recv.at[j], t_ss.at[j], t_rs.at[j], device_z(1)) for j in range(chunks)]
    u_copies = {
        (m, j): remote(u_send.at[j], u_recv.at[j], u_ss.at[m, j], u_rs.at[j], device_z(m))
        for m in (2, 3) for j in range(chunks)
    }

    def values(j):
        far_copies[j].wait_recv()
        total = acc[j] + p_recv[j, 0].astype(F32) + far_recv[j].astype(F32)
        value[j] = (total / (1.0 + jnp.exp(-total))).astype(BF16)
        for i in range(2):
            hd = 2 * j + i
            state[j, i] = lax.dot_general(
                key[:, pl.ds(hd * HD, HD)], value[j, :, pl.ds(i * HD, HD)],
                (((0,), (0,)), ((), ())), preferred_element_type=F32,
            )
        s_copies[j].start()
        for i in range(2):
            att[2 * j + i] = jnp.dot(
                scores[2 * j + i], value[j, :, pl.ds(i * HD, HD)], preferred_element_type=F32
            )

    def pair_sum(j):
        s_copies[j].wait_recv()
        pre_send[j] = jnp.zeros((HD, HD), F32)

        @pl.when(zi % 2 == 0)
        def _():
            t_send[j] = (state[j, yi] + state_in[j]).astype(BF16)
            t_copies[j].start()

    def row_sum(j):
        @pl.when(zi % 2 == 1)
        def _():
            t_copies[j].wait_recv()
            pre_send[j] = t_recv[j].astype(F32)

        @pl.when(zi == 1)
        def _():
            u_send[j] = (pre_send[j] + state[j, yi] + state_in[j]).astype(BF16)
            u_copies[2, j].start()
            u_copies[3, j].start()

    def earlier(j):
        @pl.when(zi >= 2)
        def _():
            u_copies[2, j].wait_recv()
            pre_send[j] = pre_send[j] + u_recv[j].astype(F32)

        second = yi.astype(F32)
        before = pre_send[j]
        pre[j, yi] = before + second * state_in[j]
        pre_send[j] = before + (1.0 - second) * state[j, yi]
        e_copies[j].start()

    def finish(j):
        e_copies[j].wait_recv()
        for i in range(2):
            lanes = pl.ds((2 * j + i) * HD, HD)
            whole = pre[j, i]
            high = whole.astype(BF16)
            low = (whole - high.astype(F32)).astype(BF16)
            q = query[:, lanes]
            attended = (
                att[2 * j + i]
                + jnp.dot(q, high, preferred_element_type=F32)
                + jnp.dot(q, low, preferred_element_type=F32)
            )
            mean_square = jnp.mean(attended * attended, axis=1, keepdims=True)
            out[:, lanes] = (attended * lax.rsqrt(mean_square + 1e-05) * gain[:, lanes]).astype(BF16)

    stages = (values, pair_sum, row_sum, earlier, finish)
    for step in range(chunks + len(stages) - 1):
        for lag, stage in enumerate(stages):
            if 0 <= step - lag < chunks:
                stage(step - lag)

    for copy in [*token_copies.values(), *w_copies, *x_copies.values(), *core_copies.values()]:
        copy.wait_send()
    for copy in [*p_copies, *far_copies, *s_copies, *e_copies]:
        copy.wait_send()

    @pl.when(zi % 2 == 0)
    def _():
        for copy in t_copies:
            copy.wait_send()

    @pl.when(zi == 1)
    def _():
        for copy in u_copies.values():
            copy.wait_send()


def fused(n, tokens, query, key, weight, gain):
    rows = tokens.shape[0]
    depth, width = weight.shape
    nz = n // 2
    chunks = width // CW
    dma = pltpu.SemaphoreType.DMA
    hbm = pl.BlockSpec(memory_space=pl.ANY)
    vmem = pl.BlockSpec(memory_space=pltpu.VMEM)
    return pl.pallas_call(
        functools.partial(fused_kernel, nz, chunks),
        out_shape=jax.ShapeDtypeStruct((rows, width), BF16),
        in_specs=[hbm, vmem, vmem, hbm, vmem],
        out_specs=vmem,
        scratch_shapes=[
            pltpu.VMEM((nz, rows, 2 * depth), BF16),
            pltpu.VMEM((chunks, 2 * depth, CW), BF16),
            pltpu.VMEM((chunks, 2, rows, CW), BF16),
            pltpu.VMEM((chunks, 2, rows, CW), BF16),
            pltpu.VMEM((chunks, rows, CW), F32),
            pltpu.VMEM((chunks, rows, CW), BF16),
            pltpu.VMEM((chunks, rows, CW), BF16),
            pltpu.VMEM((chunks, rows, CW), F32),
            pltpu.VMEM((2 * chunks, rows, rows), BF16),
            pltpu.VMEM((chunks, rows, CW), BF16),
            pltpu.VMEM((2 * chunks, rows, HD), F32),
            pltpu.VMEM((chunks, 2, HD, HD), F32),
            pltpu.VMEM((chunks, HD, HD), F32),
            pltpu.VMEM((chunks, HD, HD), BF16),
            pltpu.VMEM((chunks, HD, HD), BF16),
            pltpu.VMEM((chunks, HD, HD), BF16),
            pltpu.VMEM((chunks, HD, HD), BF16),
            pltpu.VMEM((chunks, HD, HD), F32),
            pltpu.VMEM((chunks, 2, HD, HD), F32),
            dma((1 + chunks,)),
            dma((chunks,)), dma((chunks,)),
            dma((nz,)), dma((nz,)),
            dma((nz,)), dma((nz,)),
            dma((2, nz)), dma((2, nz)),
            dma((chunks,)), dma((chunks,)),
            dma((chunks,)), dma((chunks,)),
            dma((chunks,)), dma((chunks,)),
            dma((chunks,)), dma((chunks,)),
            dma((nz, chunks)), dma((chunks,)),
            dma((chunks,)), dma((chunks,)),
        ],
        compiler_params=pltpu.CompilerParams(
            collective_id=0, has_side_effects=True, vmem_limit_bytes=48 << 20
        ),
    )(tokens, query, key, weight, gain.reshape(1, width))


def on_device(n, heads, tokens, query_heads, key_heads, w_value, norm_gain):
    rows = tokens.shape[0]
    depth, width = w_value.shape
    fits = n == 8 and heads == 4 and rows == BLOCK and depth % 128 == 0 and width % CW == 0
    if fits:
        return fused(n, tokens, query_heads, key_heads, w_value, norm_gain)
    return plain(tokens, query_heads, key_heads, w_value, norm_gain)


def solution(mesh):
    return jax.shard_map(
        functools.partial(on_device, mesh.shape["ctx"], mesh.shape["head"]),
        mesh=mesh,
        in_specs=(P("ctx", None), P("ctx", "head"), P("ctx", "head"), P("ctx", "head"), P("head")),
        out_specs=P("ctx", "head"),
        check_vma=False,
    )
```

```python
import functools

import jax
import jax.numpy as jnp
from jax import lax
from jax.experimental import pallas as pl
from jax.experimental.pallas import tpu as pltpu
from jax.sharding import PartitionSpec as P

MESH = pl.DeviceIdType.MESH
F32 = jnp.float32
BF16 = jnp.bfloat16
CW = 256
W_AHEAD = 2
ORDER = (1, 3, 2)

HD = 128
BLOCK = 256


def prefix(part, axis, combine, identity):
    place = lax.axis_index(axis)
    gathered = lax.all_gather(part, axis)
    state = jnp.zeros_like(part) + jnp.asarray(identity, part.dtype)

    def one(lap, state):
        return combine(state, lax.dynamic_index_in_dim(gathered, lap, 0, False))

    return lax.fori_loop(0, place, one, state)


def add_states(earlier, later):
    return earlier + later


def plain(tokens, query_heads, key_heads, w_value, norm_gain):
    token_count = tokens.shape[0]
    width = w_value.shape[1]
    heads_here = width // HD
    full_weight = lax.all_gather(w_value, "ctx", axis=0, tiled=True)
    pre_value = jnp.dot(tokens, full_weight, preferred_element_type=jnp.float32)
    value_heads = jax.nn.silu(pre_value).astype(jnp.bfloat16)
    block_count = token_count // BLOCK
    block_shape = (block_count, BLOCK, heads_here, HD)
    shaped_q = query_heads.reshape(block_shape)
    shaped_k = key_heads.reshape(block_shape)
    shaped_v = value_heads.reshape(block_shape)
    local_states = jnp.einsum(
        "bshd,bshe->bhde", shaped_k, shaped_v, preferred_element_type=jnp.float32
    )
    device_state = jnp.sum(local_states, axis=0)
    running_sum = jnp.cumsum(local_states, axis=0)
    before_block = jnp.concatenate([jnp.zeros_like(local_states), running_sum[:-1]], axis=0)
    earlier = prefix(device_state, "ctx", add_states, jnp.zeros_like(device_state))
    prefix_state = earlier[None] + before_block
    inter = jnp.einsum(
        "bshd,bhde->bshe",
        shaped_q.astype(jnp.float32),
        prefix_state,
        precision=lax.Precision.HIGHEST,
    )
    scores = jnp.einsum("bshd,bthd->bhst", shaped_q, shaped_k, preferred_element_type=jnp.float32)
    causal = jnp.tril(jnp.ones((BLOCK, BLOCK), jnp.bool_))
    scores = jnp.where(causal[None, None], scores, jnp.float32(0.0)).astype(jnp.bfloat16)
    intra = jnp.einsum("bhst,bthd->bshd", scores, shaped_v, preferred_element_type=jnp.float32)
    attended = (inter + intra).reshape(token_count, heads_here, HD)
    mean_square = jnp.mean(attended * attended, axis=2, keepdims=True)
    normed = attended * lax.rsqrt(mean_square + 1e-05) * norm_gain.reshape(1, heads_here, HD)
    return normed.reshape(token_count, width).astype(jnp.bfloat16)


def fused_kernel(
    nz, chunks, tokens, query, key, weight, gain, out,
    tok, wbuf, p_send, p_recv, far, far_send, far_recv, acc, scores, value, att,
    state, state_in, t_send, u_send, t_recv, u_recv, pre_send, pre,
    local_sem, w_ss, w_rs, tok_ss, tok_rs, x_ss, x_rs, core_ss, core_rs, p_ss, p_rs, f_ss, f_rs,
    s_ss, s_rs, t_ss, t_rs, u_ss, u_rs, e_ss, e_rs,
):
    ctx = lax.axis_index("ctx")
    head = lax.axis_index("head")
    zi, yi = ctx // 2, ctx % 2
    rows = tokens.shape[0]
    depth = weight.shape[0]
    slice_width = 2 * depth
    quarter = rows // 4

    z_peers = {1: zi + 1 - 2 * (zi % 2), 2: lax.rem(zi + 2, nz), 3: nz - 1 - zi}

    def device_z(m):
        return (z_peers[m] * 2 + yi, head)

    pair = (zi * 2 + 1 - yi, head)
    core_peer = head + 1 - 2 * (head % 2)
    x_peer = lax.rem(head + 2, 4)

    def remote(src, dst, ss, rs, device):
        return pltpu.make_async_remote_copy(
            src_ref=src, dst_ref=dst, send_sem=ss, recv_sem=rs, device_id=device, device_id_type=MESH
        )

    def columns(z):
        return pl.ds(pl.multiple_of(z * slice_width, 128), slice_width)

    def token_rows(h):
        return pl.ds(pl.multiple_of(h * quarter, quarter), quarter)

    own_rows = pl.ds(pl.multiple_of(yi * depth, depth), depth)

    own_tokens = pltpu.make_async_copy(tokens.at[:, columns(zi)], tok.at[zi], local_sem.at[0])
    own_tokens.start()
    own_weights = []
    for j in range(chunks):
        own_weights.append(
            pltpu.make_async_copy(
                weight.at[:, pl.ds(j * CW, CW)], wbuf.at[j, own_rows, :], local_sem.at[1 + j]
            )
        )
        own_weights[j].start()

    barrier = pltpu.get_barrier_semaphore()
    greeted = [device_z(m) for m in z_peers] + [pair, (ctx, core_peer), (ctx, x_peer)]
    for device in greeted:
        pl.semaphore_signal(barrier, inc=1, device_id=device, device_id_type=MESH)
    pl.semaphore_wait(barrier, len(greeted))

    w_copies = []
    for j in range(chunks):
        w_copies.append(
            remote(
                weight.at[:, pl.ds(j * CW, CW)], wbuf.at[j, own_rows, :], w_ss.at[j], w_rs.at[j], pair
            )
        )
    for j in range(min(W_AHEAD, chunks)):
        w_copies[j].start()
    token_copies = {}
    for m in ORDER:
        token_copies[m] = remote(
            tokens.at[token_rows(head), columns(z_peers[m])],
            tok.at[zi, token_rows(head), :],
            tok_ss.at[m], tok_rs.at[m], device_z(m),
        )
        token_copies[m].start()

    row = lax.broadcasted_iota(jnp.int32, (rows, rows), 0)
    column = lax.broadcasted_iota(jnp.int32, (rows, rows), 1)
    causal = column <= row
    for hd in range(2 * chunks):
        lanes = pl.ds(hd * HD, HD)
        full = lax.dot_general(
            query[:, lanes], key[:, lanes], (((1,), (1,)), ((), ())), preferred_element_type=F32
        )
        scores[hd] = jnp.where(causal, full, 0.0).astype(BF16)

    x_copies, core_copies = {}, {}
    for m in ORDER:
        mine = tok.at[z_peers[m], token_rows(head), :]
        token_copies[m].wait_recv()
        x_copies[m] = remote(mine, mine, x_ss.at[m], x_rs.at[m], (ctx, x_peer))
        x_copies[m].start()
        core_copies[m, 0] = remote(mine, mine, core_ss.at[0, m], core_rs.at[0, m], (ctx, core_peer))
        core_copies[m, 0].start()
    for m in ORDER:
        other = tok.at[z_peers[m], token_rows(x_peer), :]
        x_copies[m].wait_recv()
        core_copies[m, 1] = remote(other, other, core_ss.at[1, m], core_rs.at[1, m], (ctx, core_peer))
        core_copies[m, 1].start()

    p_copies = [remote(p_send.at[j], p_recv.at[j], p_ss.at[j], p_rs.at[j], device_z(1)) for j in range(chunks)]
    far_copies = [
        remote(far_send.at[j], far_recv.at[j], f_ss.at[j], f_rs.at[j], device_z(2)) for j in range(chunks)
    ]

    def tokens_of(m, j):
        if j == 0:
            core_copies[m, 0].wait_recv()
            core_copies[m, 1].wait_recv()
        return tok[z_peers[m]]

    def near_parts(j):
        own_weights[j].wait()
        w_copies[j].wait_recv()
        if j + W_AHEAD < chunks:
            w_copies[j + W_AHEAD].start()
        for i, m in enumerate((1, 3)):
            p_send[j, i] = jnp.dot(tokens_of(m, j), wbuf[j], preferred_element_type=F32).astype(BF16)
        p_copies[j].start()
        if j == 0:
            own_tokens.wait()
        far[j] = jnp.dot(tokens_of(2, j), wbuf[j], preferred_element_type=F32)
        acc[j] = jnp.dot(tok[zi], wbuf[j], preferred_element_type=F32)

    def far_parts(j):
        p_copies[j].wait_recv()
        far_send[j] = (far[j] + p_recv[j, 1].astype(F32)).astype(BF16)
        far_copies[j].start()

    s_copies = [
        remote(state.at[j, 1 - yi], state_in.at[j], s_ss.at[j], s_rs.at[j], pair) for j in range(chunks)
    ]
    e_copies = [
        remote(pre_send.at[j], pre.at[j, yi], e_ss.at[j], e_rs.at[j], pair) for j in range(chunks)
    ]

    t_copies = [remote(t_send.at[j], t_recv.at[j], t_ss.at[j], t_rs.at[j], device_z(1)) for j in range(chunks)]
    u_copies = {
        (m, j): remote(u_send.at[j], u_recv.at[j], u_ss.at[m, j], u_rs.at[j], device_z(m))
        for m in (2, 3) for j in range(chunks)
    }

    def values(j):
        far_copies[j].wait_recv()
        total = acc[j] + p_recv[j, 0].astype(F32) + far_recv[j].astype(F32)
        value[j] = (total / (1.0 + jnp.exp(-total))).astype(BF16)
        for i in range(2):
            hd = 2 * j + i
            state[j, i] = lax.dot_general(
                key[:, pl.ds(hd * HD, HD)], value[j, :, pl.ds(i * HD, HD)],
                (((0,), (0,)), ((), ())), preferred_element_type=F32,
            )
        s_copies[j].start()
        for i in range(2):
            att[2 * j + i] = jnp.dot(
                scores[2 * j + i], value[j, :, pl.ds(i * HD, HD)], preferred_element_type=F32
            )

    def pair_sum(j):
        s_copies[j].wait_recv()
        pre_send[j] = jnp.zeros((HD, HD), F32)

        @pl.when(zi % 2 == 0)
        def _():
            t_send[j] = (state[j, yi] + state_in[j]).astype(BF16)
            t_copies[j].start()

    def row_sum(j):
        @pl.when(zi % 2 == 1)
        def _():
            t_copies[j].wait_recv()
            pre_send[j] = t_recv[j].astype(F32)

        @pl.when(zi == 1)
        def _():
            u_send[j] = (pre_send[j] + state[j, yi] + state_in[j]).astype(BF16)
            u_copies[2, j].start()
            u_copies[3, j].start()

    def earlier(j):
        @pl.when(zi >= 2)
        def _():
            u_copies[2, j].wait_recv()
            pre_send[j] = pre_send[j] + u_recv[j].astype(F32)

        second = yi.astype(F32)
        before = pre_send[j]
        pre[j, yi] = before + second * state_in[j]
        pre_send[j] = before + (1.0 - second) * state[j, yi]
        e_copies[j].start()

    def finish(j):
        e_copies[j].wait_recv()
        for i in range(2):
            lanes = pl.ds((2 * j + i) * HD, HD)
            whole = pre[j, i]
            high = whole.astype(BF16)
            low = (whole - high.astype(F32)).astype(BF16)
            q = query[:, lanes]
            attended = (
                att[2 * j + i]
                + jnp.dot(q, high, preferred_element_type=F32)
                + jnp.dot(q, low, preferred_element_type=F32)
            )
            mean_square = jnp.mean(attended * attended, axis=1, keepdims=True)
            out[:, lanes] = (attended * lax.rsqrt(mean_square + 1e-05) * gain[:, lanes]).astype(BF16)

    stages = {near_parts: 0, far_parts: 1, values: 2, pair_sum: 3, row_sum: 4, earlier: 5, finish: 6}
    for step in range(chunks + stages[finish]):
        for stage, lag in stages.items():
            if 0 <= step - lag < chunks:
                stage(step - lag)

    for copy in [*token_copies.values(), *w_copies, *x_copies.values(), *core_copies.values()]:
        copy.wait_send()
    for copy in [*p_copies, *far_copies, *s_copies, *e_copies]:
        copy.wait_send()

    @pl.when(zi % 2 == 0)
    def _():
        for copy in t_copies:
            copy.wait_send()

    @pl.when(zi == 1)
    def _():
        for copy in u_copies.values():
            copy.wait_send()


def fused(n, tokens, query, key, weight, gain):
    rows = tokens.shape[0]
    depth, width = weight.shape
    nz = n // 2
    chunks = width // CW
    dma = pltpu.SemaphoreType.DMA
    hbm = pl.BlockSpec(memory_space=pl.ANY)
    vmem = pl.BlockSpec(memory_space=pltpu.VMEM)
    return pl.pallas_call(
        functools.partial(fused_kernel, nz, chunks),
        out_shape=jax.ShapeDtypeStruct((rows, width), BF16),
        in_specs=[hbm, vmem, vmem, hbm, vmem],
        out_specs=vmem,
        scratch_shapes=[
            pltpu.VMEM((nz, rows, 2 * depth), BF16),
            pltpu.VMEM((chunks, 2 * depth, CW), BF16),
            pltpu.VMEM((chunks, 2, rows, CW), BF16),
            pltpu.VMEM((chunks, 2, rows, CW), BF16),
            pltpu.VMEM((chunks, rows, CW), F32),
            pltpu.VMEM((chunks, rows, CW), BF16),
            pltpu.VMEM((chunks, rows, CW), BF16),
            pltpu.VMEM((chunks, rows, CW), F32),
            pltpu.VMEM((2 * chunks, rows, rows), BF16),
            pltpu.VMEM((chunks, rows, CW), BF16),
            pltpu.VMEM((2 * chunks, rows, HD), F32),
            pltpu.VMEM((chunks, 2, HD, HD), F32),
            pltpu.VMEM((chunks, HD, HD), F32),
            pltpu.VMEM((chunks, HD, HD), BF16),
            pltpu.VMEM((chunks, HD, HD), BF16),
            pltpu.VMEM((chunks, HD, HD), BF16),
            pltpu.VMEM((chunks, HD, HD), BF16),
            pltpu.VMEM((chunks, HD, HD), F32),
            pltpu.VMEM((chunks, 2, HD, HD), F32),
            dma((1 + chunks,)),
            dma((chunks,)), dma((chunks,)),
            dma((nz,)), dma((nz,)),
            dma((nz,)), dma((nz,)),
            dma((2, nz)), dma((2, nz)),
            dma((chunks,)), dma((chunks,)),
            dma((chunks,)), dma((chunks,)),
            dma((chunks,)), dma((chunks,)),
            dma((chunks,)), dma((chunks,)),
            dma((nz, chunks)), dma((chunks,)),
            dma((chunks,)), dma((chunks,)),
        ],
        compiler_params=pltpu.CompilerParams(
            collective_id=0, has_side_effects=True, vmem_limit_bytes=48 << 20
        ),
    )(tokens, query, key, weight, gain.reshape(1, width))


def on_device(n, heads, tokens, query_heads, key_heads, w_value, norm_gain):
    rows = tokens.shape[0]
    depth, width = w_value.shape
    fits = n == 8 and heads == 4 and rows == BLOCK and depth % 128 == 0 and width % CW == 0
    if fits:
        return fused(n, tokens, query_heads, key_heads, w_value, norm_gain)
    return plain(tokens, query_heads, key_heads, w_value, norm_gain)


def solution(mesh):
    return jax.shard_map(
        functools.partial(on_device, mesh.shape["ctx"], mesh.shape["head"]),
        mesh=mesh,
        in_specs=(P("ctx", None), P("ctx", "head"), P("ctx", "head"), P("ctx", "head"), P("head")),
        out_specs=P("ctx", "head"),
        check_vma=False,
    )
```
